32 devices in a mesh: pipe: 8 (over z, core), expert: 4 (over y, x).
Axes of the slice: x: 2, y: 2, z: 4, core: 2. Of those that a mesh axis runs over, the one named last changes fastest.
Arguments:
- fwd_state: bfloat16 [8, 512, 3584], P('pipe', 'expert'), may hold values from -6 to 6
- bwd_cot: bfloat16 [8, 512, 3584], P('pipe', 'expert'), may hold values from -6 to 6
- saved_inputs: bfloat16 [2, 8, 512, 3584], P(None, 'pipe', 'expert'), may hold values from -6 to 6
- fwd_entry: bfloat16 [512, 3584], P('expert'), may hold values from -6 to 6
- bwd_entry: bfloat16 [512, 3584], P('expert'), may hold values from -6 to 6
- fwd_ids: int32 [2, 8, 512, 2], P(None, 'pipe', 'expert'), may hold values from 0 to 3, all different within a row; in each aligned block of 128 rows (0 to 127, 128 to 255, ..., all dimensions but the last counted through in order) at most 80 rows name the same one
- bwd_ids: int32 [2, 8, 512, 2], P(None, 'pipe', 'expert'), may hold values from 0 to 3, all different within a row; in each aligned block of 128 rows (0 to 127, 128 to 255, ..., all dimensions but the last counted through in order) at most 80 rows name the same one
- norm_gain: float32 [8, 3584], P('pipe'), may hold values from 0.1 to 1.9
- router: bfloat16 [8, 3584, 4], P('pipe'), may hold values from -0.09375 to 0.09375
- up_weight: bfloat16 [8, 4, 3584, 1024], P('pipe', 'expert'), may hold values from -0.09375 to 0.09375
- down_weight: bfloat16 [8, 4, 1024, 3584], P('pipe', 'expert'), may hold values from -0.1875 to 0.1875
Outputs:
- fwd_out: bfloat16 [2, 8, 512, 3584], P(None, 'pipe', 'expert')
- bwd_out: bfloat16 [2, 8, 512, 3584], P(None, 'pipe', 'expert')
The draws below stay inside these ranges and needn't reach their ends.
Inputs may be any that keep to these rules, and one draw needn't show every extreme that they name: `fwd_ids`: the 2 ids of a token differ. Within the 128 tokens of one device (aligned blocks), no expert is named by more than 80 tokens, a bound that some block reaches. `bwd_ids`: as for fwd_ids.
All inputs are finite; a program needn't handle non-finite values.
Results may differ from the reference program's by a relative error of at most 0.0059.
Values may be sent and summed in bfloat16 or wider, within the bound.
A program may use at most 128 MiB of HBM per device.

```python
import math
import jax
import jax.numpy as jnp
import numpy as np
from jax import lax

D = 3584
F = 1024
TOPK = 2
TICKS = 2
TOK_DEV = 128
LAYERS = 8
EXPERTS = 4
TOKENS = 512
CAP = 80
N_EXPERT = 4


def steps_of(key, extent, split, least, top_value):
    loudness, own = 1.0, jax.random.fold_in(key, 6)
    for axis_at, blocks in split:
        draws = jnp.exp(jax.random.uniform(jax.random.fold_in(own, axis_at), (blocks,), jnp.float32, least / len(split), top_value / len(split)))
        loudness = loudness * jnp.repeat(draws, extent[axis_at] // blocks).reshape([-1 if axis == axis_at else 1 for axis in range(len(extent))])
    return loudness


def shared_out(key, own, number, rows, count, top, reach, lean):
    order = jax.random.permutation(key, count)
    crowded, common = portions_of(count, rows * top, reach, lean, True), portions_of(count, rows * top, reach, lean, False)
    places = jnp.arange(count)

    def named(sizes, offset_by):
        used = int((sizes > 0).sum())
        fixed = max(1, used // 4)
        shifted = fixed + (places - fixed + offset_by * (used - fixed)) % max(1, count - fixed)
        return jnp.zeros((count,), jnp.int32).at[order[jnp.where(places < fixed, places, shifted)]].set(jnp.asarray(sizes, jnp.int32))

    sizes = jnp.where(number % 4 == 0, named(crowded, number // 4), named(common, number - number // 4 - 1))
    mixed = jax.random.permutation(jax.random.fold_in(own, 3), count)
    donor, taker = mixed[0:count // 2 * 2:2], mixed[1:count // 2 * 2:2]
    room = jnp.minimum(sizes[donor] - 1, reach - sizes[taker]) // 2
    room = jnp.where((donor == order[0]) | (taker == order[0]) | (sizes[taker] == 0), 0, jnp.maximum(room, 0))
    shifted = jax.random.randint(jax.random.fold_in(own, 4), (count // 2,), 0, 1 << 20) % (room + 1)
    sizes = sizes.at[donor].add(-shifted).at[taker].add(shifted)
    labels = jnp.searchsorted(jnp.cumsum(sizes), jnp.arange(rows * top), side="right").astype(jnp.int32)
    grid = labels.reshape(top, rows).T
    grid = grid[jax.random.permutation(jax.random.fold_in(own, 1), rows)]
    offset_by = jax.random.randint(jax.random.fold_in(own, 2), (rows, 1), 0, top)
    return jnp.take_along_axis(grid, (jnp.arange(top)[None, :] + offset_by) % top, axis=1)


def portions_of(count, total, bound, slope, full):
    weights = [(1 << 20) // math.isqrt(rank ** slope) + 1 for rank in range(1, count + 1)]
    largest = bound if full else min(bound, max(-(-total // count), total * weights[0] // sum(weights)))
    least = 1 if total - largest >= count - 1 else 0
    counts, rest = [largest] + [least] * (count - 1), total - largest - least * (count - 1)
    while rest > 0:
        candidates = [i for i in range(1, count) if counts[i] < largest] or [i for i in range(1, count) if counts[i] < bound]
        pool, left = sum([weights[i] for i in candidates]), rest
        for i in candidates:
            more = min(bound - counts[i], max(1, left * weights[i] // pool), rest)
            counts[i] = counts[i] + more
            rest = rest - more
    return np.array(counts)


def gaussian(key, shape, scale, bound, cuts=(), held_as=jnp.bfloat16):
    values = scale * jax.random.normal(key, shape, jnp.float32)
    if cuts:
        values = values * steps_of(key, shape, cuts, -0.22, 0.18)
    return jnp.clip(values, -bound, bound).astype(held_as)


def setup_inputs(seed: int = 0) -> dict:
    streams_of = jax.random.split(jax.random.key(seed), 12)
    fwd_state = gaussian(streams_of[0], (LAYERS, TOKENS, D), 1.0, 6.0, ((0, 8), (1, 4)))
    bwd_cot = gaussian(streams_of[1], (LAYERS, TOKENS, D), 1.0, 6.0, ((0, 8), (1, 4)))
    saved_inputs = gaussian(streams_of[2], (TICKS, LAYERS, TOKENS, D), 1.0, 6.0, ((1, 8), (2, 4)))
    fwd_entry = gaussian(streams_of[3], (TOKENS, D), 1.0, 6.0, ((0, 4),))
    bwd_entry = gaussian(streams_of[4], (TOKENS, D), 1.0, 6.0, ((0, 4),))
    fwd_ids_keys = jax.random.split(jax.random.fold_in(streams_of[5], 1), TICKS * LAYERS * TOKENS // TOK_DEV)
    fwd_ids_turns = jax.random.permutation(jax.random.fold_in(streams_of[5], 3), TICKS * LAYERS * TOKENS // TOK_DEV)
    fwd_ids = jax.vmap(lambda own, number: shared_out(jax.random.fold_in(streams_of[5], 2), own, number, TOK_DEV, EXPERTS, TOPK, CAP, 2))(fwd_ids_keys, fwd_ids_turns).reshape((TICKS, LAYERS, TOKENS, TOPK))
    bwd_ids_keys = jax.random.split(jax.random.fold_in(streams_of[6], 1), TICKS * LAYERS * TOKENS // TOK_DEV)
    bwd_ids_turns = jax.random.permutation(jax.random.fold_in(streams_of[6], 3), TICKS * LAYERS * TOKENS // TOK_DEV)
    bwd_ids = jax.vmap(lambda own, number: shared_out(jax.random.fold_in(streams_of[6], 2), own, number, TOK_DEV, EXPERTS, TOPK, CAP, 2))(bwd_ids_keys, bwd_ids_turns).reshape((TICKS, LAYERS, TOKENS, TOPK))
    norm_gain = jnp.clip(1.0 + 0.18 * jax.random.normal(streams_of[7], (LAYERS, D), jnp.float32), 0.1, 1.9)
    router = gaussian(streams_of[8], (LAYERS, D, EXPERTS), D ** -0.5, 0.09375, ((0, 8),))
    up_weight = gaussian(streams_of[9], (LAYERS, EXPERTS, D, F), D ** -0.5, 0.09375, ((0, 8), (1, 4)))
    down_weight = gaussian(streams_of[10], (LAYERS, EXPERTS, F, D), F ** -0.5, 0.1875, ((0, 8), (1, 4)))
    return dict(fwd_state=fwd_state, bwd_cot=bwd_cot, saved_inputs=saved_inputs, fwd_entry=fwd_entry, bwd_entry=bwd_entry, fwd_ids=fwd_ids, bwd_ids=bwd_ids, norm_gain=norm_gain, router=router, up_weight=up_weight, down_weight=down_weight)


EPSILON = 1e-06

def normalize(activation, gain_row):
    values = activation.astype(jnp.float32)
    inverse_rms = lax.rsqrt(lax.optimization_barrier(jnp.mean(values * values, axis=-1, keepdims=True)) + EPSILON)
    return ((values * inverse_rms * gain_row).astype(jnp.bfloat16), inverse_rms)

def gating(normed, routing, expert_ids):
    logits = jnp.dot(normed, routing, preferred_element_type=jnp.float32)
    probability = jax.nn.sigmoid(logits)
    picked = expert_ids[:, :, None] == jnp.arange(routing.shape[1], dtype=jnp.int32)[None, None, :]
    chosen = lax.optimization_barrier(jnp.sum(jnp.where(picked, probability[:, None, :], 0.0), axis=-1))
    chosen_sum = lax.optimization_barrier(jnp.sum(chosen, axis=-1, keepdims=True))
    return (chosen / chosen_sum, chosen, chosen_sum, picked)

def expert_forward(row_block, up_matrix, down_matrix):
    upward = jnp.dot(row_block, up_matrix, preferred_element_type=jnp.float32)
    hidden = (upward * jax.nn.sigmoid(upward)).astype(jnp.bfloat16)
    return jnp.dot(hidden, down_matrix, preferred_element_type=jnp.float32).astype(jnp.bfloat16)

def expert_backward(row_block, gradients, up_matrix, down_matrix):
    upward = jnp.dot(row_block, up_matrix, preferred_element_type=jnp.float32)
    sigmoid_up = jax.nn.sigmoid(upward)
    hidden = (upward * sigmoid_up).astype(jnp.bfloat16)
    outputs = jnp.dot(hidden, down_matrix, preferred_element_type=jnp.float32).astype(jnp.bfloat16)
    dhidden = lax.dot_general(gradients, down_matrix, (((1,), (1,)), ((), ())), preferred_element_type=jnp.float32)
    dupward = (dhidden * sigmoid_up * (1.0 + upward * (1.0 - sigmoid_up))).astype(jnp.bfloat16)
    dnormed = lax.dot_general(dupward, up_matrix, (((1,), (1,)), ((), ())), preferred_element_type=jnp.float32)
    return (outputs, dnormed.astype(jnp.bfloat16))

def finish_backward(activation, cotangent, inverse_rms, gain_row, routing, gate_weight, chosen, chosen_sum, picked, expert_out, expert_grad):
    cot_values = cotangent.astype(jnp.float32)
    gate_grad = lax.optimization_barrier(jnp.sum(cot_values[:, None, :] * expert_out.astype(jnp.float32), axis=-1))
    chosen_grad = (gate_grad - lax.optimization_barrier(jnp.sum(gate_grad * gate_weight, axis=-1, keepdims=True))) / chosen_sum
    selected_grad = chosen_grad * chosen * (1.0 - chosen)
    logit_grad = lax.optimization_barrier(jnp.sum(jnp.where(picked, selected_grad[:, :, None], 0.0), axis=1))
    router_part = jnp.dot(logit_grad, routing.astype(jnp.float32).T, precision=lax.Precision.HIGHEST)
    norm_grad = lax.optimization_barrier(jnp.sum(expert_grad.astype(jnp.float32), axis=1)) + router_part
    scaled_grad = norm_grad * gain_row
    values = activation.astype(jnp.float32)
    correction = lax.optimization_barrier(jnp.mean(scaled_grad * values, axis=-1, keepdims=True))
    result = cot_values + inverse_rms * scaled_grad - values * inverse_rms ** 3 * correction
    return result.astype(jnp.bfloat16)

def reference(fwd_state, bwd_cot, saved_inputs, fwd_entry, bwd_entry, fwd_ids, bwd_ids, norm_gain, router, up_weight, down_weight):
    per_expert = N_EXPERT * CAP
    assignments = TOKENS * TOPK
    token_of = jnp.arange(assignments, dtype=jnp.int32) // TOPK

    def route_rows(expert_ids):
        flattened = expert_ids.reshape(assignments)
        onehot = (flattened[:, None] == jnp.arange(EXPERTS, dtype=jnp.int32)[None, :]).astype(jnp.int32)
        position = lax.optimization_barrier(jnp.sum((jnp.cumsum(onehot, axis=0) - 1) * onehot, axis=1))
        return (flattened * per_expert + position).astype(jnp.int32)

    def scatter_rows(rows, slot_index):
        buffer = jnp.zeros((EXPERTS * per_expert, D), jnp.bfloat16).at[slot_index].set(rows)
        return buffer.reshape(EXPERTS, per_expert, D)

    def layer_forward(operands):
        activation, gain_row, routing, up_matrix, down_matrix, expert_ids = operands
        normed, inverse_rms = normalize(activation, gain_row)
        gate_weight, chosen, chosen_sum, picked = gating(normed, routing, expert_ids)
        slot_index = route_rows(expert_ids)
        buffer = scatter_rows(normed[token_of], slot_index)
        results = lax.map(lambda parts: expert_forward(parts[0], parts[1], parts[2]), (buffer, up_matrix, down_matrix))
        expert_out = results.reshape(EXPERTS * per_expert, D)[slot_index].reshape(TOKENS, TOPK, D)
        mixed = activation.astype(jnp.float32) + lax.optimization_barrier(jnp.sum(gate_weight[:, :, None] * expert_out.astype(jnp.float32), axis=1))
        return mixed.astype(jnp.bfloat16)

    def layer_backward(operands):
        activation, cotangent, gain_row, routing, up_matrix, down_matrix, expert_ids = operands
        normed, inverse_rms = normalize(activation, gain_row)
        gate_weight, chosen, chosen_sum, picked = gating(normed, routing, expert_ids)
        out_grad = (gate_weight[:, :, None] * cotangent.astype(jnp.float32)[:, None, :]).astype(jnp.bfloat16)
        slot_index = route_rows(expert_ids)
        row_buffer = scatter_rows(normed[token_of], slot_index)
        grad_buffer = scatter_rows(out_grad.reshape(assignments, D), slot_index)
        outputs, dnormed = lax.map(lambda parts: expert_backward(parts[0], parts[1], parts[2], parts[3]), (row_buffer, grad_buffer, up_matrix, down_matrix))
        expert_out = outputs.reshape(EXPERTS * per_expert, D)[slot_index].reshape(TOKENS, TOPK, D)
        expert_grad = dnormed.reshape(EXPERTS * per_expert, D)[slot_index].reshape(TOKENS, TOPK, D)
        return finish_backward(activation, cotangent, inverse_rms, gain_row, routing, gate_weight, chosen, chosen_sum, picked, expert_out, expert_grad)
    forward_in = fwd_state
    cotangent_in = bwd_cot
    forward_list = []
    backward_list = []
    for tick_number in range(TICKS):
        forward_result = lax.map(layer_forward, (forward_in, norm_gain, router, up_weight, down_weight, fwd_ids[tick_number]))
        backward_result = lax.map(layer_backward, (saved_inputs[tick_number], cotangent_in, norm_gain, router, up_weight, down_weight, bwd_ids[tick_number]))
        forward_list.append(forward_result)
        backward_list.append(backward_result)
        forward_in = jnp.concatenate([fwd_entry[None], forward_result[:-1]], axis=0)
        cotangent_in = jnp.concatenate([backward_result[1:], bwd_entry[None]], axis=0)
    return (jnp.stack(forward_list), jnp.stack(backward_list))
```

```python
import functools

import jax
import jax.numpy as jnp
from jax import lax
from jax.experimental import pallas as pl
from jax.experimental.pallas import tpu as pltpu
from jax.sharding import PartitionSpec as P

EPSILON = 1e-06
LANES = 128
F32 = jnp.float32
BF16 = jnp.bfloat16
NN = (((1,), (0,)), ((), ()))
NT = (((1,), (1,)), ((), ()))


def mm(a, b, dims=NN, precision=None):
    return lax.dot_general(a, b, dims, preferred_element_type=F32, precision=precision)


def tile_of(extent, most):
    size = most
    while extent % size:
        size -= LANES
    return size


def window_kernel(
    sections,
    experts,
    capacity,
    fwd_state,
    bwd_cot,
    saved,
    fwd_entry,
    bwd_entry,
    fwd_ids,
    fwd_ids_t,
    bwd_ids,
    bwd_ids_t,
    gain,
    router_t,
    up_hbm,
    down_hbm,
    fwd_out,
    bwd_out,
    up_w,
    down_w,
    acts,
    cots,
    stored,
    send_f,
    send_s,
    send_c,
    recv_f,
    recv_s,
    recv_c,
    ret_f,
    ret_g,
    gate_send,
    gate_ret,
    up_buf,
    hid_buf,
    dup_buf,
    scaled_buf,
    load_sems,
    send_sems,
    recv_sems,
    own_sems,
    pipe_send,
    pipe_recv,
    out_sems,
):
    ticks, tokens, width = saved.shape
    top_count = fwd_ids.shape[2]
    hidden_width = up_w.shape[1]
    rows = experts * capacity
    section = lax.axis_index("pipe")
    me = lax.axis_index("expert")
    wide = tile_of(width, 512)
    wide_count = width // wide
    narrow = tile_of(hidden_width, 256)
    narrow_count = hidden_width // narrow

    loads = [
        pltpu.make_async_copy(fwd_state, acts.at[0], load_sems.at[0]),
        pltpu.make_async_copy(bwd_cot, cots.at[0], load_sems.at[1]),
        pltpu.make_async_copy(saved, stored, load_sems.at[2]),
        pltpu.make_async_copy(up_hbm, up_w, load_sems.at[3]),
        pltpu.make_async_copy(down_hbm, down_w, load_sems.at[4]),
    ]
    for load in loads:
        load.start()

    barrier = pltpu.get_barrier_semaphore()
    for offset in range(1, experts):
        pl.semaphore_signal(
            barrier,
            inc=1,
            device_id=(section, lax.rem(me + offset, experts)),
            device_id_type=pl.DeviceIdType.MESH,
        )
    for offset in (1, sections - 1):
        pl.semaphore_signal(
            barrier,
            inc=1,
            device_id=(lax.rem(section + offset, sections), me),
            device_id_type=pl.DeviceIdType.MESH,
        )

    def block_of(index):
        return pl.ds(pl.multiple_of(index * capacity, 16), capacity)

    def exchange(source, target, tick, channel):
        own = pltpu.make_async_copy(
            source.at[block_of(me)], target.at[block_of(me)], own_sems.at[tick, channel]
        )
        copies = []
        for offset in range(1, experts):
            peer = lax.rem(me + offset, experts)
            copies.append(
                pltpu.make_async_remote_copy(
                    src_ref=source.at[block_of(peer)],
                    dst_ref=target.at[block_of(me)],
                    send_sem=send_sems.at[tick, channel, offset - 1],
                    recv_sem=recv_sems.at[tick, channel, offset - 1],
                    device_id=(section, peer),
                    device_id_type=pl.DeviceIdType.MESH,
                )
            )
        for copy in copies:
            copy.start()
        own.start()
        return own, copies

    def arrived(pair):
        pair[0].wait()
        for copy in pair[1]:
            copy.wait_recv()

    def sent(pair):
        for copy in pair[1]:
            copy.wait_send()

    def wide_at(step):
        return pl.ds(pl.multiple_of(step * wide, LANES), wide)

    def narrow_at(step):
        return pl.ds(pl.multiple_of(step * narrow, LANES), narrow)

    def folded(value):
        return sum(value[:, i : i + LANES] for i in range(0, value.shape[1], LANES))

    before = lax.broadcasted_iota(jnp.int32, (tokens, tokens), 0)
    after = lax.broadcasted_iota(jnp.int32, (tokens, tokens), 1)
    lower = jnp.where(after < before, 1.0, 0.0).astype(BF16)
    upper = jnp.where(before < after, 1.0, 0.0).astype(BF16)

    def slots_of(ids_ref, tick):
        ids = ids_ref[tick]
        lane = lax.broadcasted_iota(jnp.int32, (tokens, LANES), 1)
        member = sum(jnp.where(ids[:, k : k + 1] == lane, 1.0, 0.0) for k in range(top_count))
        position = mm(lower, member.astype(BF16))
        base = lane.astype(F32) * float(capacity)
        return member, jnp.where(member > 0.5, position + base, -1.0)

    def packing(ids_t_ref, tick):
        ids = ids_t_ref[tick]
        level = lax.broadcasted_iota(jnp.int32, (16, tokens), 0)
        member = sum(jnp.where(ids[k : k + 1, :] == level, 1.0, 0.0) for k in range(top_count))
        position = mm(member.astype(BF16), upper)
        base = level.astype(F32) * float(capacity)
        slot = jnp.where(member > 0.5, position + base, -1.0)
        row = lax.broadcasted_iota(jnp.int32, (rows, tokens), 0).astype(F32)
        picked = sum(jnp.where(row == slot[e : e + 1, :], 1.0, 0.0) for e in range(experts))
        return picked.astype(BF16)

    def unpacking(slot, weight):
        row = lax.broadcasted_iota(jnp.int32, (tokens, rows), 1).astype(F32)
        return sum(
            jnp.where(row == slot[:, e : e + 1], weight[:, e : e + 1], 0.0)
            for e in range(experts)
        )

    def split_stack(matrix):
        high = matrix.astype(BF16)
        low = (matrix - high.astype(F32)).astype(BF16)
        return jnp.concatenate([high, low], axis=0)

    def inverse_of(act):
        def body(step, total):
            values = act[:, wide_at(step)].astype(F32)
            return total + folded(values * values)

        total = lax.fori_loop(0, wide_count, body, jnp.zeros((tokens, LANES), F32))
        mean = jnp.sum(total, axis=-1, keepdims=True) / float(width)
        return lax.rsqrt(mean + EPSILON)

    def normed_pack(act, inverse, pick, target):
        def body(step, logits):
            at = wide_at(step)
            normed = (act[:, at].astype(F32) * inverse * gain[:, at]).astype(BF16)
            target[:, at] = mm(pick, normed).astype(BF16)
            return logits + mm(normed, router_t[:, at], NT)

        return lax.fori_loop(0, wide_count, body, jnp.zeros((tokens, LANES), F32))

    def plain_pack(act, pick, target):
        def body(step, carry):
            at = wide_at(step)
            target[:, at] = mm(pick, act[:, at]).astype(BF16)
            return carry

        lax.fori_loop(0, wide_count, body, 0)

    def gating(logits, member):
        probability = jax.nn.sigmoid(logits)
        chosen = jnp.where(member > 0.5, probability, 0.0)
        chosen_sum = jnp.sum(chosen, axis=-1, keepdims=True)
        return chosen / chosen_sum, probability, chosen_sum

    def expert_forward(block):
        def up_body(step, carry):
            at = narrow_at(step)
            upward = mm(block[...], up_w[:, at])
            hid_buf[:, at] = (upward * jax.nn.sigmoid(upward)).astype(BF16)
            return carry

        lax.fori_loop(0, narrow_count, up_body, 0)

        def down_body(step, carry):
            at = wide_at(step)
            block[:, at] = mm(hid_buf[...], down_w[:, at]).astype(BF16)
            return carry

        lax.fori_loop(0, wide_count, down_body, 0)

    def expert_up(block):
        def body(step, carry):
            at = narrow_at(step)
            up_buf[:, at] = mm(block[...], up_w[:, at])
            return carry

        lax.fori_loop(0, narrow_count, body, 0)

    def expert_backward(cot_block, target, tick):
        def body(step, total):
            at = narrow_at(step)
            grad = mm(cot_block[...], down_w[at, :], NT)
            upward = up_buf[:, at]
            gate = jax.nn.sigmoid(upward)
            hidden = (upward * gate).astype(BF16).astype(F32)
            dup_buf[:, at] = (grad * gate * (1.0 + upward * (1.0 - gate))).astype(BF16)
            return total + folded(hidden * grad)

        total = lax.fori_loop(0, narrow_count, body, jnp.zeros((rows, LANES), F32))
        gate_grad = jnp.sum(total, axis=-1, keepdims=True)
        lane = lax.broadcasted_iota(jnp.int32, (rows, LANES), 1)
        gate_send[tick] = jnp.where(lane == me, gate_grad, 0.0)

        def back_body(step, carry):
            at = wide_at(step)
            target[:, at] = mm(dup_buf[...], up_w[at, :], NT).astype(BF16)
            return carry

        lax.fori_loop(0, wide_count, back_body, 0)

    def finish_forward(act, back, stack):
        def body(step, carry):
            at = wide_at(step)
            both = mm(stack, back[:, at])
            mixed = act[:, at].astype(F32) + (both[:tokens] + both[tokens:])
            act[:, at] = mixed.astype(BF16)
            return carry

        lax.fori_loop(0, wide_count, body, 0)

    def finish_backward(cot, source, back, gate_back, slot, member, gates, inverse):
        gate, probability, chosen_sum = gates
        stack = split_stack(unpacking(slot, gate))
        plain = unpacking(slot, member)
        gate_grad = mm(plain, gate_back[...], NN, lax.Precision.HIGHEST)
        inner = jnp.sum(gate_grad * gate, axis=-1, keepdims=True)
        chosen_grad = (gate_grad - inner) / chosen_sum
        logit_grad = jnp.where(
            member > 0.5, chosen_grad * probability * (1.0 - probability), 0.0
        )

        def body(step, total):
            at = wide_at(step)
            both = mm(stack, back[:, at])
            grad = both[:tokens] + both[tokens:]
            routing = router_t[0:16, at].astype(F32)
            for e in range(experts):
                grad = grad + logit_grad[:, e : e + 1] * routing[e : e + 1, :]
            scaled = grad * gain[:, at]
            scaled_buf[:, at] = scaled
            return total + folded(scaled * source[:, at].astype(F32))

        total = lax.fori_loop(0, wide_count, body, jnp.zeros((tokens, LANES), F32))
        correction = jnp.sum(total, axis=-1, keepdims=True) / float(width)
        factor = inverse * inverse * inverse * correction

        def last_body(step, carry):
            at = wide_at(step)
            values = source[:, at].astype(F32)
            result = cot[:, at].astype(F32) + inverse * scaled_buf[:, at] - values * factor
            cot[:, at] = result.astype(BF16)
            return carry

        lax.fori_loop(0, wide_count, last_body, 0)

    def start_forward(tick):
        act = acts.at[tick]
        inverse = inverse_of(act)
        logits = normed_pack(act, inverse, packing(fwd_ids_t, tick), send_f)
        return logits

    def forward_stack(tick, logits):
        member, slot = slots_of(fwd_ids, tick)
        gate, _, _ = gating(logits, member)
        return split_stack(unpacking(slot, gate))

    def start_stored(tick):
        act = stored.at[tick]
        inverse = inverse_of(act)
        logits = normed_pack(act, inverse, packing(bwd_ids_t, tick), send_s)
        return inverse, logits

    def end_backward(tick, inverse, logits):
        member, slot = slots_of(bwd_ids, tick)
        gates = gating(logits, member)
        finish_backward(
            cots.at[tick],
            stored.at[tick],
            ret_g,
            gate_ret,
            slot,
            member,
            gates,
            inverse,
        )

    loads[0].wait()
    logits_f = start_forward(0)
    pl.semaphore_wait(barrier, experts + 1)
    trip_f = exchange(send_f, recv_f.at[0], 0, 0)
    loads[2].wait()
    inverse_s, logits_s = start_stored(0)
    trip_s = exchange(send_s, recv_s.at[0], 0, 1)
    loads[1].wait()
    plain_pack(cots.at[0], packing(bwd_ids_t, 0), send_c)
    trip_c = exchange(send_c, recv_c, 0, 2)
    loads[3].wait()
    loads[4].wait()

    outs = []
    for tick in range(ticks):
        more = tick + 1 < ticks
        arrived(trip_f)
        expert_forward(recv_f.at[tick])
        back_f = exchange(recv_f.at[tick], ret_f, tick, 3)
        if tick == 0:
            arrived(trip_s)
            expert_up(recv_s.at[tick])
        arrived(trip_c)
        expert_backward(recv_c, recv_s.at[tick], tick)
        back_g = exchange(recv_s.at[tick], ret_g, tick, 4)
        back_w = exchange(gate_send.at[tick], gate_ret, tick, 5)
        sent(trip_s)
        sent(trip_f)
        sent(trip_c)
        this_inverse, this_logits = inverse_s, logits_s
        if more:
            inverse_s, logits_s = start_stored(tick + 1)
            trip_s = exchange(send_s, recv_s.at[tick + 1], tick + 1, 1)

        arrived(back_f)
        finish_forward(acts.at[tick], ret_f, forward_stack(tick, logits_f))
        outs.append(pltpu.make_async_copy(acts.at[tick], fwd_out.at[tick], out_sems.at[tick, 0]))
        outs[-1].start()
        if more:
            up_hop = pltpu.make_async_remote_copy(
                src_ref=acts.at[tick],
                dst_ref=acts.at[tick + 1],
                send_sem=pipe_send.at[tick, 0],
                recv_sem=pipe_recv.at[tick, 0],
                device_id=(jnp.minimum(section + 1, sections - 1), me),
                device_id_type=pl.DeviceIdType.MESH,
            )
            entry_f = pltpu.make_async_copy(fwd_entry, acts.at[tick + 1], load_sems.at[5])
            pl.when(section < sections - 1)(up_hop.start)
            pl.when(section == 0)(entry_f.start)

        arrived(back_g)
        arrived(back_w)
        end_backward(tick, this_inverse, this_logits)
        outs.append(pltpu.make_async_copy(cots.at[tick], bwd_out.at[tick], out_sems.at[tick, 1]))
        outs[-1].start()
        if more:
            down_hop = pltpu.make_async_remote_copy(
                src_ref=cots.at[tick],
                dst_ref=cots.at[tick + 1],
                send_sem=pipe_send.at[tick, 1],
                recv_sem=pipe_recv.at[tick, 1],
                device_id=(jnp.maximum(section - 1, 0), me),
                device_id_type=pl.DeviceIdType.MESH,
            )
            entry_b = pltpu.make_async_copy(bwd_entry, cots.at[tick + 1], load_sems.at[6])
            pl.when(section > 0)(down_hop.start)
            pl.when(section == sections - 1)(entry_b.start)

            pl.when(section > 0)(up_hop.wait_recv)
            pl.when(section == 0)(entry_f.wait)
            logits_f = start_forward(tick + 1)
            trip_f = exchange(send_f, recv_f.at[tick + 1], tick + 1, 0)
            pl.when(section < sections - 1)(down_hop.wait_recv)
            pl.when(section == sections - 1)(entry_b.wait)
            plain_pack(cots.at[tick + 1], packing(bwd_ids_t, tick + 1), send_c)
            trip_c = exchange(send_c, recv_c, tick + 1, 2)
            arrived(trip_s)
            expert_up(recv_s.at[tick + 1])
            pl.when(section < sections - 1)(up_hop.wait_send)
            pl.when(section > 0)(down_hop.wait_send)
        sent(back_f)
        sent(back_g)
        sent(back_w)
    for out in outs:
        out.wait()


def per_device(
    fwd_state,
    bwd_cot,
    saved_inputs,
    fwd_entry,
    bwd_entry,
    fwd_ids,
    bwd_ids,
    norm_gain,
    router,
    up_weight,
    down_weight,
):
    sections = lax.axis_size("pipe")
    experts = lax.axis_size("expert")
    ticks, _, tokens, width = saved_inputs.shape
    top_count = fwd_ids.shape[3]
    hidden_width = up_weight.shape[3]
    capacity = -(-(5 * tokens * top_count // (4 * experts)) // 16) * 16
    rows = experts * capacity
    router_t = jnp.pad(router[0].T, ((0, LANES - experts), (0, 0)))
    fwd_route, bwd_route = fwd_ids[:, 0], bwd_ids[:, 0]
    anywhere = pl.BlockSpec(memory_space=pl.ANY)
    near = pl.BlockSpec(memory_space=pltpu.VMEM)
    out = jax.ShapeDtypeStruct((ticks, tokens, width), BF16)
    wide_block = pltpu.VMEM((rows, width), BF16)
    tick_block = pltpu.VMEM((ticks, rows, width), BF16)
    token_block = pltpu.VMEM((ticks, tokens, width), BF16)
    small_block = pltpu.VMEM((ticks, rows, LANES), F32)
    forward, backward = pl.pallas_call(
        functools.partial(window_kernel, sections, experts, capacity),
        name="relay_window",
        out_shape=(out, out),
        in_specs=[anywhere] * 5 + [near] * 6 + [anywhere] * 2,
        out_specs=(anywhere, anywhere),
        scratch_shapes=[
            pltpu.VMEM((width, hidden_width), BF16),
            pltpu.VMEM((hidden_width, width), BF16),
            token_block,
            token_block,
            token_block,
            wide_block,
            wide_block,
            wide_block,
            tick_block,
            tick_block,
            wide_block,
            wide_block,
            wide_block,
            small_block,
            pltpu.VMEM((rows, LANES), F32),
            pltpu.VMEM((rows, hidden_width), F32),
            pltpu.VMEM((rows, hidden_width), BF16),
            pltpu.VMEM((rows, hidden_width), BF16),
            pltpu.VMEM((tokens, width), F32),
            pltpu.SemaphoreType.DMA((7,)),
            pltpu.SemaphoreType.DMA((ticks, 6, experts - 1)),
            pltpu.SemaphoreType.DMA((ticks, 6, experts - 1)),
            pltpu.SemaphoreType.DMA((ticks, 6)),
            pltpu.SemaphoreType.DMA((ticks, 2)),
            pltpu.SemaphoreType.DMA((ticks, 2)),
            pltpu.SemaphoreType.DMA((ticks, 2)),
        ],
        compiler_params=pltpu.CompilerParams(
            collective_id=0, has_side_effects=True, vmem_limit_bytes=63 * 1024 * 1024
        ),
    )(
        fwd_state[0],
        bwd_cot[0],
        saved_inputs[:, 0],
        fwd_entry,
        bwd_entry,
        fwd_route,
        jnp.swapaxes(fwd_route, 1, 2),
        bwd_route,
        jnp.swapaxes(bwd_route, 1, 2),
        norm_gain,
        router_t,
        up_weight[0, 0],
        down_weight[0, 0],
    )
    return forward[:, None], backward[:, None]


def solution(mesh):
    placed = (
        P("pipe", "expert", None),
        P("pipe", "expert", None),
        P(None, "pipe", "expert", None),
        P("expert", None),
        P("expert", None),
        P(None, "pipe", "expert", None),
        P(None, "pipe", "expert", None),
        P("pipe", None),
        P("pipe", None, None),
        P("pipe", "expert", None, None),
        P("pipe", "expert", None, None),
    )
    return jax.shard_map(
        per_device,
        mesh=mesh,
        in_specs=placed,
        out_specs=(P(None, "pipe", "expert", None), P(None, "pipe", "expert", None)),
        check_vma=False,
    )
```

```python
import functools

import jax
import jax.numpy as jnp
from jax import lax
from jax.experimental import pallas as pl
from jax.experimental.pallas import tpu as pltpu
from jax.sharding import PartitionSpec as P

EPSILON = 1e-06
LANES = 128
F32 = jnp.float32
BF16 = jnp.bfloat16
NN = (((1,), (0,)), ((), ()))
NT = (((1,), (1,)), ((), ()))


def mm(a, b, dims=NN, precision=None):
    return lax.dot_general(a, b, dims, preferred_element_type=F32, precision=precision)


def tile_of(extent, most):
    size = most
    while extent % size:
        size -= LANES
    return size


def window_kernel(
    sections,
    experts,
    capacity,
    fwd_state,
    bwd_cot,
    saved,
    fwd_entry,
    bwd_entry,
    fwd_ids,
    fwd_ids_t,
    bwd_ids,
    bwd_ids_t,
    gain,
    router_t,
    up_hbm,
    down_hbm,
    fwd_out,
    bwd_out,
    up_w,
    down_w,
    acts,
    cots,
    stored,
    send_f,
    send_s,
    send_c,
    recv_f,
    recv_s,
    recv_c,
    ret_f,
    ret_g,
    gate_send,
    gate_ret,
    up_buf,
    hid_buf,
    dup_buf,
    scaled_buf,
    load_sems,
    send_sems,
    recv_sems,
    own_sems,
    pipe_send,
    pipe_recv,
    out_sems,
):
    ticks, tokens, width = saved.shape
    top_count = fwd_ids.shape[2]
    hidden_width = up_w.shape[1]
    rows = experts * capacity
    section = lax.axis_index("pipe")
    me = lax.axis_index("expert")
    wide = tile_of(width, 512)
    wide_count = width // wide
    narrow = tile_of(hidden_width, 256)
    narrow_count = hidden_width // narrow

    loads = [
        pltpu.make_async_copy(fwd_state, acts.at[0], load_sems.at[0]),
        pltpu.make_async_copy(bwd_cot, cots.at[0], load_sems.at[1]),
        pltpu.make_async_copy(saved, stored, load_sems.at[2]),
        pltpu.make_async_copy(up_hbm, up_w, load_sems.at[3]),
        pltpu.make_async_copy(down_hbm, down_w, load_sems.at[4]),
    ]
    for load in loads:
        load.start()

    barrier = pltpu.get_barrier_semaphore()
    for offset in range(1, experts):
        pl.semaphore_signal(
            barrier,
            inc=1,
            device_id=(section, lax.rem(me + offset, experts)),
            device_id_type=pl.DeviceIdType.MESH,
        )
    for offset in (1, sections - 1):
        pl.semaphore_signal(
            barrier,
            inc=1,
            device_id=(lax.rem(section + offset, sections), me),
            device_id_type=pl.DeviceIdType.MESH,
        )

    def block_of(index):
        return pl.ds(pl.multiple_of(index * capacity, 16), capacity)

    def exchange(source, target, tick, channel, at=None, view=None):
        view = view or (lambda ref, index: ref.at[block_of(index), at or slice(0, width)])
        own = pltpu.make_async_copy(
            view(source, me), view(target, me), own_sems.at[tick, channel]
        )
        copies = []
        for offset in range(1, experts):
            peer = lax.rem(me + offset, experts)
            copies.append(
                pltpu.make_async_remote_copy(
                    src_ref=view(source, peer),
                    dst_ref=view(target, me),
                    send_sem=send_sems.at[tick, channel, offset - 1],
                    recv_sem=recv_sems.at[tick, channel, offset - 1],
                    device_id=(section, peer),
                    device_id_type=pl.DeviceIdType.MESH,
                )
            )
        for copy in copies:
            copy.start()
        own.start()
        return own, copies

    def arrived(pair):
        pair[0].wait()
        for copy in pair[1]:
            copy.wait_recv()

    def sent(pair):
        for copy in pair[1]:
            copy.wait_send()

    def wide_at(step):
        return pl.ds(pl.multiple_of(step * wide, LANES), wide)

    def narrow_at(step):
        return pl.ds(pl.multiple_of(step * narrow, LANES), narrow)

    def folded(value):
        return sum(value[:, i : i + LANES] for i in range(0, value.shape[1], LANES))

    before = lax.broadcasted_iota(jnp.int32, (tokens, tokens), 0)
    after = lax.broadcasted_iota(jnp.int32, (tokens, tokens), 1)
    lower = jnp.where(after < before, 1.0, 0.0).astype(BF16)
    upper = jnp.where(before < after, 1.0, 0.0).astype(BF16)

    def slots_of(ids_ref, tick):
        ids = ids_ref[tick]
        lane = lax.broadcasted_iota(jnp.int32, (tokens, LANES), 1)
        member = sum(jnp.where(ids[:, k : k + 1] == lane, 1.0, 0.0) for k in range(top_count))
        position = mm(lower, member.astype(BF16))
        base = lane.astype(F32) * float(capacity)
        return (
            member,
            jnp.where(member > 0.5, position + base, -1.0),
            jnp.where(member > 0.5, position, -1.0),
        )

    def packing(ids_t_ref, tick):
        ids = ids_t_ref[tick]
        level = lax.broadcasted_iota(jnp.int32, (16, tokens), 0)
        member = sum(jnp.where(ids[k : k + 1, :] == level, 1.0, 0.0) for k in range(top_count))
        position = mm(member.astype(BF16), upper)
        base = level.astype(F32) * float(capacity)
        slot = jnp.where(member > 0.5, position + base, -1.0)
        row = lax.broadcasted_iota(jnp.int32, (rows, tokens), 0).astype(F32)
        picked = sum(jnp.where(row == slot[e : e + 1, :], 1.0, 0.0) for e in range(experts))
        return picked.astype(BF16)

    def unpacking(slot, weight):
        row = lax.broadcasted_iota(jnp.int32, (tokens, rows), 1).astype(F32)
        return sum(
            jnp.where(row == slot[:, e : e + 1], weight[:, e : e + 1], 0.0)
            for e in range(experts)
        )

    def split_stack(matrix):
        high = matrix.astype(BF16)
        low = (matrix - high.astype(F32)).astype(BF16)
        return jnp.concatenate([high, low], axis=0)

    def inverse_of(act):
        def body(step, total):
            values = act[:, wide_at(step)].astype(F32)
            return total + folded(values * values)

        total = lax.fori_loop(0, wide_count, body, jnp.zeros((tokens, LANES), F32))
        mean = jnp.sum(total, axis=-1, keepdims=True) / float(width)
        return lax.rsqrt(mean + EPSILON)

    def normed_pack(act, inverse, pick, target):
        def body(step, logits):
            at = wide_at(step)
            normed = (act[:, at].astype(F32) * inverse * gain[:, at]).astype(BF16)
            target[:, at] = mm(pick, normed).astype(BF16)
            return logits + mm(normed, router_t[:, at], NT)

        return lax.fori_loop(0, wide_count, body, jnp.zeros((tokens, LANES), F32))

    def plain_pack(act, pick, target):
        def body(step, carry):
            at = wide_at(step)
            target[:, at] = mm(pick, act[:, at]).astype(BF16)
            return carry

        lax.fori_loop(0, wide_count, body, 0)

    def gating(logits, member):
        probability = jax.nn.sigmoid(logits)
        chosen = jnp.where(member > 0.5, probability, 0.0)
        chosen_sum = jnp.sum(chosen, axis=-1, keepdims=True)
        return chosen / chosen_sum, probability, chosen_sum

    def expert_forward(block):
        def up_body(step, carry):
            at = narrow_at(step)
            upward = mm(block[...], up_w[:, at])
            hid_buf[:, at] = (upward * jax.nn.sigmoid(upward)).astype(BF16)
            return carry

        lax.fori_loop(0, narrow_count, up_body, 0)

        def down_body(step, carry):
            at = wide_at(step)
            block[:, at] = mm(hid_buf[...], down_w[:, at]).astype(BF16)
            return carry

        lax.fori_loop(0, wide_count, down_body, 0)

    def expert_up(block):
        def body(step, carry):
            at = narrow_at(step)
            up_buf[:, at] = mm(block[...], up_w[:, at])
            return carry

        lax.fori_loop(0, narrow_count, body, 0)

    def expert_backward(cot_block, tick):
        def body(step, total):
            at = narrow_at(step)
            grad = mm(cot_block[...], down_w[at, :], NT)
            upward = up_buf[:, at]
            gate = jax.nn.sigmoid(upward)
            hidden = (upward * gate).astype(BF16).astype(F32)
            dup_buf[:, at] = (grad * gate * (1.0 + upward * (1.0 - gate))).astype(BF16)
            return total + folded(hidden * grad)

        total = lax.fori_loop(0, narrow_count, body, jnp.zeros((rows, LANES), F32))
        ones = jnp.ones((8, LANES), F32)
        for source in range(experts):
            part = total[source * capacity : (source + 1) * capacity]
            gate_send[tick, source] = jnp.zeros((8, LANES), F32)
            gate_send[tick, source, :, 0:capacity] = mm(ones, part, NT, lax.Precision.HIGHEST)

        def back_body(step, carry):
            at = wide_at(step)
            recv_s[tick, :, at] = mm(dup_buf[...], up_w[at, :], NT).astype(BF16)
            return carry

        return back_body

    def expert_return(body, target, tick):
        cuts = [0, (wide_count + 1) // 2, wide_count]
        trips = []
        for part in range(2):
            lax.fori_loop(cuts[part], cuts[part + 1], body, 0)
            at = slice(cuts[part] * wide, cuts[part + 1] * wide)
            if at.stop > at.start:
                trips.append(exchange(target, ret_g, tick, 4 + part, at))
        return trips

    def finish_forward(act, back, stack):
        def body(step, carry):
            at = wide_at(step)
            both = mm(stack, back[:, at])
            mixed = act[:, at].astype(F32) + (both[:tokens] + both[tokens:])
            act[:, at] = mixed.astype(BF16)
            return carry

        lax.fori_loop(0, wide_count, body, 0)

    def finish_backward(cot, source, back, gate_back, ready):
        stack, member, position, gates, inverse = ready
        gate, probability, chosen_sum = gates
        lane = lax.broadcasted_iota(jnp.int32, (tokens, LANES), 1)
        gate_grad = jnp.zeros((tokens, LANES), F32)
        for e in range(experts):
            named = jnp.where(lane.astype(F32) == position[:, e : e + 1], gate_back[e, 0:1, :], 0.0)
            value = jnp.sum(named, axis=-1, keepdims=True)
            gate_grad = jnp.where(lane == e, value, gate_grad)
        inner = jnp.sum(gate_grad * gate, axis=-1, keepdims=True)
        chosen_grad = (gate_grad - inner) / chosen_sum
        logit_grad = jnp.where(
            member > 0.5, chosen_grad * probability * (1.0 - probability), 0.0
        )

        def body(step, total):
            at = wide_at(step)
            both = mm(stack, back[:, at])
            grad = both[:tokens] + both[tokens:]
            routing = router_t[0:16, at].astype(F32)
            for e in range(experts):
                grad = grad + logit_grad[:, e : e + 1] * routing[e : e + 1, :]
            scaled = grad * gain[:, at]
            scaled_buf[:, at] = scaled
            return total + folded(scaled * source[:, at].astype(F32))

        total = lax.fori_loop(0, wide_count, body, jnp.zeros((tokens, LANES), F32))
        correction = jnp.sum(total, axis=-1, keepdims=True) / float(width)
        factor = inverse * inverse * inverse * correction

        def last_body(step, carry):
            at = wide_at(step)
            values = source[:, at].astype(F32)
            result = cot[:, at].astype(F32) + inverse * scaled_buf[:, at] - values * factor
            cot[:, at] = result.astype(BF16)
            return carry

        lax.fori_loop(0, wide_count, last_body, 0)

    def start_forward(tick):
        act = acts.at[tick]
        inverse = inverse_of(act)
        logits = normed_pack(act, inverse, packing(fwd_ids_t, tick), send_f)
        return logits

    def forward_ready(tick, logits):
        member, slot, _ = slots_of(fwd_ids, tick)
        gate, _, _ = gating(logits, member)
        return split_stack(unpacking(slot, gate))

    def start_stored(tick):
        act = stored.at[tick]
        inverse = inverse_of(act)
        logits = normed_pack(act, inverse, packing(bwd_ids_t, tick), send_s)
        return inverse, logits

    def backward_ready(tick, inverse, logits):
        member, slot, position = slots_of(bwd_ids, tick)
        gates = gating(logits, member)
        return split_stack(unpacking(slot, gates[0])), member, position, gates, inverse

    loads[0].wait()
    logits_f = start_forward(0)
    pl.semaphore_wait(barrier, experts + 1)
    trip_f = exchange(send_f, recv_f.at[0], 0, 0)
    loads[2].wait()
    inverse_s, logits_s = start_stored(0)
    trip_s = exchange(send_s, recv_s.at[0], 0, 1)
    loads[1].wait()
    plain_pack(cots.at[0], packing(bwd_ids_t, 0), send_c)
    trip_c = exchange(send_c, recv_c, 0, 2)
    loads[3].wait()
    loads[4].wait()

    def own_row(ref, index):
        return ref.at[index]

    outs = []
    for tick in range(ticks):
        more = tick + 1 < ticks
        act, cot = acts.at[tick], cots.at[tick]
        arrived(trip_f)
        expert_forward(recv_f.at[tick])
        if more:
            back_f = exchange(recv_f.at[tick], ret_f, tick, 3)
        arrived(trip_s)
        expert_up(recv_s.at[tick])
        stack_f = forward_ready(tick, logits_f)
        ready_b = backward_ready(tick, inverse_s, logits_s)
        arrived(trip_c)
        if not more:
            back_f = exchange(recv_f.at[tick], ret_f, tick, 3)
        body = expert_backward(recv_c, tick)
        back_w = exchange(gate_send.at[tick], gate_ret, tick, 6, view=own_row)
        back_g = expert_return(body, recv_s.at[tick], tick)
        sent(trip_s)
        sent(trip_f)
        sent(trip_c)
        if more:
            inverse_s, logits_s = start_stored(tick + 1)

        arrived(back_f)
        finish_forward(act, ret_f, stack_f)
        if more:
            up_hop = pltpu.make_async_remote_copy(
                src_ref=act,
                dst_ref=acts.at[tick + 1],
                send_sem=pipe_send.at[tick, 0],
                recv_sem=pipe_recv.at[tick, 0],
                device_id=(jnp.minimum(section + 1, sections - 1), me),
                device_id_type=pl.DeviceIdType.MESH,
            )
            entry_f = pltpu.make_async_copy(fwd_entry, acts.at[tick + 1], load_sems.at[5])
            pl.when(section < sections - 1)(up_hop.start)
            pl.when(section == 0)(entry_f.start)
        outs.append(pltpu.make_async_copy(act, fwd_out.at[tick], out_sems.at[tick, 0]))
        outs[-1].start()
        if more:
            pl.when(section > 0)(up_hop.wait_recv)
            pl.when(section == 0)(entry_f.wait)
            logits_f = start_forward(tick + 1)
            trip_f = exchange(send_f, recv_f.at[tick + 1], tick + 1, 0)

        for part in back_g:
            arrived(part)
        arrived(back_w)
        if more:
            trip_s = exchange(send_s, recv_s.at[tick + 1], tick + 1, 1)
        finish_backward(cot, stored.at[tick], ret_g, gate_ret, ready_b)
        if more:
            down_hop = pltpu.make_async_remote_copy(
                src_ref=cot,
                dst_ref=cots.at[tick + 1],
                send_sem=pipe_send.at[tick, 1],
                recv_sem=pipe_recv.at[tick, 1],
                device_id=(jnp.maximum(section - 1, 0), me),
                device_id_type=pl.DeviceIdType.MESH,
            )
            entry_b = pltpu.make_async_copy(bwd_entry, cots.at[tick + 1], load_sems.at[6])
            pl.when(section > 0)(down_hop.start)
            pl.when(section == sections - 1)(entry_b.start)
        outs.append(pltpu.make_async_copy(cot, bwd_out.at[tick], out_sems.at[tick, 1]))
        outs[-1].start()
        if more:
            pl.when(section < sections - 1)(down_hop.wait_recv)
            pl.when(section == sections - 1)(entry_b.wait)
            plain_pack(cots.at[tick + 1], packing(bwd_ids_t, tick + 1), send_c)
            trip_c = exchange(send_c, recv_c, tick + 1, 2)
            pl.when(section < sections - 1)(up_hop.wait_send)
            pl.when(section > 0)(down_hop.wait_send)
        sent(back_f)
        for part in back_g:
            sent(part)
        sent(back_w)
    for out in outs:
        out.wait()


def per_device(
    fwd_state,
    bwd_cot,
    saved_inputs,
    fwd_entry,
    bwd_entry,
    fwd_ids,
    bwd_ids,
    norm_gain,
    router,
    up_weight,
    down_weight,
):
    sections = lax.axis_size("pipe")
    experts = lax.axis_size("expert")
    ticks, _, tokens, width = saved_inputs.shape
    top_count = fwd_ids.shape[3]
    hidden_width = up_weight.shape[3]
    capacity = -(-(5 * tokens * top_count // (4 * experts)) // 16) * 16
    rows = experts * capacity
    router_t = jnp.pad(router[0].T, ((0, LANES - experts), (0, 0)))
    fwd_route, bwd_route = fwd_ids[:, 0], bwd_ids[:, 0]
    anywhere = pl.BlockSpec(memory_space=pl.ANY)
    near = pl.BlockSpec(memory_space=pltpu.VMEM)
    out = jax.ShapeDtypeStruct((ticks, tokens, width), BF16)
    wide_block = pltpu.VMEM((rows, width), BF16)
    tick_block = pltpu.VMEM((ticks, rows, width), BF16)
    token_block = pltpu.VMEM((ticks, tokens, width), BF16)
    small_block = pltpu.VMEM((ticks, experts, 8, LANES), F32)
    forward, backward = pl.pallas_call(
        functools.partial(window_kernel, sections, experts, capacity),
        name="relay_window",
        out_shape=(out, out),
        in_specs=[anywhere] * 5 + [near] * 6 + [anywhere] * 2,
        out_specs=(anywhere, anywhere),
        scratch_shapes=[
            pltpu.VMEM((width, hidden_width), BF16),
            pltpu.VMEM((hidden_width, width), BF16),
            token_block,
            token_block,
            token_block,
            wide_block,
            wide_block,
            wide_block,
            tick_block,
            tick_block,
            wide_block,
            wide_block,
            wide_block,
            small_block,
            pltpu.VMEM((experts, 8, LANES), F32),
            pltpu.VMEM((rows, hidden_width), F32),
            pltpu.VMEM((rows, hidden_width), BF16),
            pltpu.VMEM((rows, hidden_width), BF16),
            pltpu.VMEM((tokens, width), F32),
            pltpu.SemaphoreType.DMA((7,)),
            pltpu.SemaphoreType.DMA((ticks, 7, experts - 1)),
            pltpu.SemaphoreType.DMA((ticks, 7, experts - 1)),
            pltpu.SemaphoreType.DMA((ticks, 7)),
            pltpu.SemaphoreType.DMA((ticks, 2)),
            pltpu.SemaphoreType.DMA((ticks, 2)),
            pltpu.SemaphoreType.DMA((ticks, 2)),
        ],
        compiler_params=pltpu.CompilerParams(
            collective_id=0, has_side_effects=True, vmem_limit_bytes=63 * 1024 * 1024
        ),
    )(
        fwd_state[0],
        bwd_cot[0],
        saved_inputs[:, 0],
        fwd_entry,
        bwd_entry,
        fwd_route,
        jnp.swapaxes(fwd_route, 1, 2),
        bwd_route,
        jnp.swapaxes(bwd_route, 1, 2),
        norm_gain,
        router_t,
        up_weight[0, 0],
        down_weight[0, 0],
    )
    return forward[:, None], backward[:, None]


def solution(mesh):
    placed = (
        P("pipe", "expert", None),
        P("pipe", "expert", None),
        P(None, "pipe", "expert", None),
        P("expert", None),
        P("expert", None),
        P(None, "pipe", "expert", None),
        P(None, "pipe", "expert", None),
        P("pipe", None),
        P("pipe", None, None),
        P("pipe", "expert", None, None),
        P("pipe", "expert", None, None),
    )
    return jax.shard_map(
        per_device,
        mesh=mesh,
        in_specs=placed,
        out_specs=(P(None, "pipe", "expert", None), P(None, "pipe", "expert", None)),
        check_vma=False,
    )
```
